128 devices in a mesh: seq: 32 (over y_lo, x, z), head: 4 (over y_hi, core).
Axes of the slice: x: 4, y: 4 (y_hi: 2, y_lo: 2; y = y_hi * 2 + y_lo), z: 4, core: 2. Of those that a mesh axis runs over, the one named last changes fastest.
Arguments:
- queries: bfloat16 [16384, 4096], P(('seq', 'head')), may hold values from -8 to 8
- keys: bfloat16 [16384, 2048], P(('seq', 'head')), may hold values from -8 to 8
- values: bfloat16 [16384, 2048], P(('seq', 'head')), may hold values from -6 to 6
- output_cotangent: bfloat16 [16384, 4096], P(('seq', 'head')), may hold values from -6 to 6
Outputs:
- attended: bfloat16 [16384, 4096], P(('seq', 'head'))
- grad_queries: bfloat16 [16384, 4096], P(('seq', 'head'))
- key_gradient: bfloat16 [16384, 2048], P(('seq', 'head'))
- value_gradient: bfloat16 [16384, 2048], P(('seq', 'head'))
The draws below stay inside these ranges and needn't reach their ends.
All inputs are finite; a program needn't handle non-finite values.
Results may differ from the reference program's by a relative error of at most 0.0095.
Values may be sent and summed in bfloat16 or wider, within the bound.
No kernel may reach another device: no remote copies, remote signals or barrier semaphores. Data moves between devices by JAX's collectives and lax.ppermute only.
A program may use at most 128 MiB of HBM per device.

```python
import jax
import jax.numpy as jnp
from jax import lax

QUERY_HEADS = 32
KEY_VALUE_HEADS = 16
HEAD_SIZE = 128
WINDOW_TOKENS = 1024
TOK_SEQ = 512
SLAB_TOKENS = 16384


def draw_pair(key):
    base = jax.random.fold_in(key, 11)
    key_q, key_rows_local = jax.random.split(base, 2)
    query_entries = jnp.clip(jax.random.normal(key_q, (SLAB_TOKENS, QUERY_HEADS, HEAD_SIZE), jnp.float32), -6.0, 6.0)
    key_entries = jnp.clip(jax.random.normal(key_rows_local, (SLAB_TOKENS, KEY_VALUE_HEADS, HEAD_SIZE), jnp.float32), -6.0, 6.0)
    query_entries = jnp.clip(query_entries, -8.0, 8.0)
    key_entries = jnp.clip(key_entries, -8.0, 8.0)
    return (query_entries.reshape(SLAB_TOKENS, QUERY_HEADS * HEAD_SIZE), key_entries.reshape(SLAB_TOKENS, KEY_VALUE_HEADS * HEAD_SIZE))


def draw_queries(key, part):
    return draw_pair(key)[0].astype(jnp.bfloat16)


def draw_keys(key, part):
    return draw_pair(key)[1].astype(jnp.bfloat16)


def level_of(own_key, dims, pieces, smallest, largest):
    level, own = 1.0, jax.random.fold_in(own_key, 6)
    for axis_at, shards_of in pieces:
        steps = jnp.exp(jax.random.uniform(jax.random.fold_in(own, axis_at), (shards_of,), jnp.float32, smallest / len(pieces), largest / len(pieces)))
        level = level * jnp.repeat(steps, dims[axis_at] // shards_of).reshape([-1 if axis == axis_at else 1 for axis in range(len(dims))])
    return level


def bell_draw(own_key, shape, deviation, most, cuts=(), kind=jnp.bfloat16):
    entries = jax.random.normal(own_key, shape, jnp.float32) * deviation
    if len(cuts) > 0:
        entries = level_of(own_key, shape, cuts, -0.22, 0.18) * entries
    return jnp.clip(entries, min=-most, max=most).astype(kind)


def setup_inputs(seed: int = 0) -> dict:
    key_list = jax.random.split(jax.random.key(seed), 5)
    return {
        "queries": draw_queries(jax.random.fold_in(key_list[4], 71), 0),
        "keys": draw_keys(jax.random.fold_in(key_list[4], 71), 0),
        "values": bell_draw(key_list[2], (SLAB_TOKENS, KEY_VALUE_HEADS * HEAD_SIZE), 1.0, 6.0, ((0, 128),)),
        "output_cotangent": bell_draw(key_list[3], (SLAB_TOKENS, QUERY_HEADS * HEAD_SIZE), 1.0, 6.0, ((0, 128),)),
    }


query_scale = 168.0 ** -0.5


def mix(form, left, right):
    return jnp.einsum(form, left.astype(jnp.float32), right.astype(jnp.float32))


def head_pass(query_head, key_extended, value_extended, grad_head, start, block):
    group_factor, total_count, width = query_head.shape
    steps = total_count // block
    rows = jnp.arange(block, dtype=jnp.int32)[:, None]
    cols = jnp.arange(WINDOW_TOKENS + block, dtype=jnp.int32)[None, :]

    def visit(carry, index):
        dk_acc, dv_acc = carry
        anchor = index * block
        query_blk = lax.dynamic_slice_in_dim(query_head, anchor, block, 1)
        grad_blk = lax.dynamic_slice_in_dim(grad_head, anchor, block, 1)
        key_slab = lax.dynamic_slice_in_dim(key_extended, anchor, WINDOW_TOKENS + block, 0)
        value_slab = lax.dynamic_slice_in_dim(value_extended, anchor, WINDOW_TOKENS + block, 0)
        key_pos = start + anchor + cols - WINDOW_TOKENS
        allowed = (cols > rows) & (cols <= rows + WINDOW_TOKENS) & (key_pos >= 0)
        scores = query_scale * mix("rqd,kd->rqk", query_blk, key_slab)
        scores = jnp.where(allowed[None], scores, -1e30)
        top = jnp.max(scores, axis=-1, keepdims=True)
        lse = top + jnp.log(jnp.sum(jnp.exp(scores - top), axis=-1, keepdims=True))
        probs = jnp.exp(scores - lse)
        probs_b = probs.astype(jnp.bfloat16)
        out_b = mix("rqk,kd->rqd", probs_b, value_slab).astype(jnp.bfloat16)
        delta = jnp.sum(grad_blk.astype(jnp.float32) * out_b.astype(jnp.float32), axis=-1)
        dprobs = mix("rqd,kd->rqk", grad_blk, value_slab)
        dscores = (probs * (dprobs - delta[..., None])).astype(jnp.bfloat16)
        dq_b = (query_scale * mix("rqk,kd->rqd", dscores, key_slab)).astype(jnp.bfloat16)
        dk_slab = query_scale * mix("rqk,rqd->kd", dscores, query_blk)
        dv_slab = mix("rqk,rqd->kd", probs_b, grad_blk)
        dk_acc = lax.dynamic_update_slice_in_dim(dk_acc, lax.dynamic_slice_in_dim(dk_acc, anchor, WINDOW_TOKENS + block, 0) + dk_slab, anchor, 0)
        dv_acc = lax.dynamic_update_slice_in_dim(dv_acc, lax.dynamic_slice_in_dim(dv_acc, anchor, WINDOW_TOKENS + block, 0) + dv_slab, anchor, 0)
        return (dk_acc, dv_acc), (out_b, dq_b)

    empty = jnp.zeros((WINDOW_TOKENS + total_count, width), jnp.float32)
    (dk_acc, dv_acc), (outs, grads) = lax.scan(visit, (empty, empty), jnp.arange(steps, dtype=jnp.int32))
    outs = outs.transpose(1, 0, 2, 3).reshape(group_factor, total_count, width)
    grads = grads.transpose(1, 0, 2, 3).reshape(group_factor, total_count, width)
    return outs, grads, dk_acc, dv_acc


def reference(queries, keys, values, output_cotangent):
    total_count = queries.shape[0]
    group_factor = QUERY_HEADS // KEY_VALUE_HEADS
    block = min(512, TOK_SEQ)
    query_head_rows = queries.reshape(total_count, KEY_VALUE_HEADS, group_factor, HEAD_SIZE).transpose(1, 2, 0, 3)
    head_gradients = output_cotangent.reshape(total_count, KEY_VALUE_HEADS, group_factor, HEAD_SIZE).transpose(1, 2, 0, 3)
    leading_part = jnp.zeros((WINDOW_TOKENS, KEY_VALUE_HEADS * HEAD_SIZE), keys.dtype)
    key_extended = jnp.concatenate([leading_part, keys], 0).reshape(WINDOW_TOKENS + total_count, KEY_VALUE_HEADS, HEAD_SIZE).transpose(1, 0, 2)
    value_extended = jnp.concatenate([leading_part, values], 0).reshape(WINDOW_TOKENS + total_count, KEY_VALUE_HEADS, HEAD_SIZE).transpose(1, 0, 2)

    def per_head(parts):
        return head_pass(parts[0], parts[1], parts[2], parts[3], 0, block)

    outs, grads_q, key_grad_parts, value_grad_parts = lax.map(per_head, (query_head_rows, key_extended, value_extended, head_gradients))
    attended = outs.transpose(2, 0, 1, 3).reshape(total_count, QUERY_HEADS * HEAD_SIZE)
    grad_queries = grads_q.transpose(2, 0, 1, 3).reshape(total_count, QUERY_HEADS * HEAD_SIZE)
    key_gradient = key_grad_parts[:, WINDOW_TOKENS:].transpose(1, 0, 2).reshape(total_count, KEY_VALUE_HEADS * HEAD_SIZE).astype(jnp.bfloat16)
    value_gradient = value_grad_parts[:, WINDOW_TOKENS:].transpose(1, 0, 2).reshape(total_count, KEY_VALUE_HEADS * HEAD_SIZE).astype(jnp.bfloat16)
    return (attended, grad_queries, key_gradient, value_gradient)
```

```python
import functools

import jax
import jax.numpy as jnp
from jax import lax
from jax.experimental import pallas as pl
from jax.experimental.pallas import tpu as pltpu
from jax.sharding import Mesh, PartitionSpec as P

D = 128
WINDOW = 1024
BLOCK = 256
CHUNKS = WINDOW // BLOCK
SCALE = 168.0 ** (-0.5)
LOG2E = 1.4426950408889634
NEG = -1e30


def cost(flops, bytes_accessed, transcendentals=0):
    return pl.CostEstimate(flops=int(flops), bytes_accessed=int(bytes_accessed), transcendentals=int(transcendentals))


def pack(arrays, widths, heads, step=4):
    rows = arrays[0].shape[0]
    total = sum(widths)

    def kernel(*refs):
        out = refs[-1]
        for j in range(step):
            at = 0
            for ref, w in zip(refs[:-1], widths):
                out[j, :, at : at + w] = ref[:, j * w : (j + 1) * w]
                at += w

    return pl.pallas_call(
        kernel,
        grid=(heads // step,),
        in_specs=[pl.BlockSpec((rows, step * w), lambda i: (0, i)) for w in widths],
        out_specs=pl.BlockSpec((step, rows, total), lambda i: (i, 0, 0)),
        out_shape=jax.ShapeDtypeStruct((heads, rows, total), arrays[0].dtype),
        cost_estimate=cost(0, 4 * heads * rows * total),
        name="pack",
    )(*arrays)


def unpack(packed, widths, step=4):
    heads, rows, total = packed.shape

    def kernel(*refs):
        src = refs[0]
        for j in range(step):
            at = 0
            for ref, w in zip(refs[1:], widths):
                ref[:, j * w : (j + 1) * w] = src[j, :, at : at + w]
                at += w

    return pl.pallas_call(
        kernel,
        grid=(heads // step,),
        in_specs=[pl.BlockSpec((step, rows, total), lambda i: (i, 0, 0))],
        out_specs=[pl.BlockSpec((rows, step * w), lambda i: (0, i)) for w in widths],
        out_shape=[jax.ShapeDtypeStruct((rows, heads * w), packed.dtype) for w in widths],
        cost_estimate=cost(0, 4 * heads * rows * total),
        name="unpack",
    )(packed)


def dot(a, b, ca, cb):
    return lax.dot_general(a, b, (((ca,), (cb,)), ((), ())), preferred_element_type=jnp.float32)


def attention_kernel(factor, first_ref, qg_ref, kv_ref, halo_ref, od_ref, dkv_ref, back_ref, kx, acc_k, acc_v, sems):
    tokens = qg_ref.shape[0]
    own = pltpu.make_async_copy(kv_ref, kx.at[pl.ds(WINDOW, tokens)], sems.at[0])
    halo = pltpu.make_async_copy(halo_ref, kx.at[pl.ds(0, WINDOW)], sems.at[1])
    own.start()
    halo.start()
    acc_k[...] = jnp.zeros_like(acc_k)
    acc_v[...] = jnp.zeros_like(acc_v)
    own.wait()
    halo.wait()
    first = first_ref[0]
    span = WINDOW + BLOCK
    row = lax.broadcasted_iota(jnp.int32, (BLOCK, BLOCK), 0)
    col = lax.broadcasted_iota(jnp.int32, (BLOCK, BLOCK), 1)
    old = col > row

    @pl.loop(0, tokens // BLOCK)
    def _(b):
        r0 = pl.multiple_of(b * BLOCK, BLOCK)
        keys = kx[pl.ds(r0, span), 0:D]
        values = kx[pl.ds(r0, span), D : 2 * D]
        hide = [jnp.where((first == 1) & (b + c < CHUNKS), 1e30, 0.0).astype(jnp.float32) for c in range(CHUNKS)]
        probs_all, ds_all, q_all, g_all = [], [], [], []
        for h in range(factor):
            q = qg_ref[pl.ds(r0, BLOCK), h * D : (h + 1) * D]
            g = qg_ref[pl.ds(r0, BLOCK), (factor + h) * D : (factor + h + 1) * D]
            s = dot(q, keys, 1, 1)
            parts = [jnp.where(old, s[:, 0:BLOCK] - hide[0], s[:, WINDOW:span])]
            parts += [s[:, c * BLOCK : (c + 1) * BLOCK] for c in range(1, CHUNKS)]
            top = jnp.max(parts[0], axis=-1, keepdims=True)
            for c in range(1, CHUNKS):
                top = jnp.maximum(top, jnp.max(parts[c], axis=-1, keepdims=True) - hide[c])
            top = top * (SCALE * LOG2E)
            es = [jnp.exp2(parts[0] * (SCALE * LOG2E) - top)]
            es += [jnp.exp2(parts[c] * (SCALE * LOG2E) - (top + hide[c])) for c in range(1, CHUNKS)]
            norm = jnp.sum(es[0] + es[1] + es[2] + es[3], axis=-1, keepdims=True)
            inv = 1.0 / norm
            ps = [e * inv for e in es]
            pb0 = ps[0].astype(jnp.bfloat16)
            zero = jnp.zeros_like(pb0)
            pb = jnp.concatenate(
                [jnp.where(old, pb0, zero)] + [p.astype(jnp.bfloat16) for p in ps[1:]] + [jnp.where(old, zero, pb0)], axis=1
            )
            out = dot(pb, values, 1, 0).astype(jnp.bfloat16)
            delta = jnp.sum(g.astype(jnp.float32) * out.astype(jnp.float32), axis=-1, keepdims=True)
            dp = dot(g, values, 1, 1)
            dparts = [jnp.where(old, dp[:, 0:BLOCK], dp[:, WINDOW:span])]
            dparts += [dp[:, c * BLOCK : (c + 1) * BLOCK] for c in range(1, CHUNKS)]
            dss = [(p * (x - delta)).astype(jnp.bfloat16) for p, x in zip(ps, dparts)]
            ds = jnp.concatenate([jnp.where(old, dss[0], zero)] + dss[1:] + [jnp.where(old, zero, dss[0])], axis=1)
            od_ref[pl.ds(r0, BLOCK), h * D : (h + 1) * D] = out
            dq = dot(ds, keys, 1, 0) * SCALE
            od_ref[pl.ds(r0, BLOCK), (factor + h) * D : (factor + h + 1) * D] = dq.astype(jnp.bfloat16)
            probs_all.append(pb)
            ds_all.append(ds)
            q_all.append(q)
            g_all.append(g)
        dk = dot(jnp.concatenate(ds_all, 0), jnp.concatenate(q_all, 0), 0, 0)
        dv = dot(jnp.concatenate(probs_all, 0), jnp.concatenate(g_all, 0), 0, 0)
        acc_k[pl.ds(r0, span), :] += dk
        acc_v[pl.ds(r0, span), :] += dv

    dkv_ref[:, 0:D] = acc_k[WINDOW:, :] * SCALE
    dkv_ref[:, D : 2 * D] = acc_v[WINDOW:, :]
    back_ref[:, 0:D] = (acc_k[:WINDOW, :] * SCALE).astype(back_ref.dtype)
    back_ref[:, D : 2 * D] = acc_v[:WINDOW, :].astype(back_ref.dtype)


def attention(first, qg, kv, halo):
    tokens = qg.shape[0]
    factor = qg.shape[1] // (2 * D)
    vmem = pl.BlockSpec(memory_space=pltpu.VMEM)
    pairs = factor * tokens * (WINDOW + BLOCK)
    return pl.pallas_call(
        functools.partial(attention_kernel, factor),
        in_specs=[pl.BlockSpec(memory_space=pltpu.SMEM), vmem, pl.BlockSpec(memory_space=pl.ANY), pl.BlockSpec(memory_space=pl.ANY)],
        out_specs=[vmem, vmem, vmem],
        out_shape=[
            jax.ShapeDtypeStruct((tokens, 2 * factor * D), jnp.bfloat16),
            jax.ShapeDtypeStruct((tokens, 2 * D), jnp.float32),
            jax.ShapeDtypeStruct((WINDOW, 2 * D), jnp.bfloat16),
        ],
        scratch_shapes=[
            pltpu.VMEM((WINDOW + tokens, 2 * D), jnp.bfloat16),
            pltpu.VMEM((WINDOW + tokens, D), jnp.float32),
            pltpu.VMEM((WINDOW + tokens, D), jnp.float32),
            pltpu.SemaphoreType.DMA((2,)),
        ],
        compiler_params=pltpu.CompilerParams(vmem_limit_bytes=56 * 1024 * 1024),
        cost_estimate=cost(12 * pairs * D, 12e6, pairs),
        name="attention",
    )(first, qg, kv, halo)


def body(queries, keys, values, output_cotangent):
    axes = ("row", "head")
    heads = lax.axis_size("row") * lax.axis_size("head")
    rows = queries.shape[0]
    wide = queries.shape[1] // heads
    slim = keys.shape[1] // heads
    groups = lax.axis_size("group")
    first = (lax.axis_index("group") == 0).astype(jnp.int32).reshape(1)

    def spread(x):
        return lax.all_to_all(x, axes, split_axis=0, concat_axis=0, tiled=True)

    kv = spread(pack([keys, values], [slim, slim], heads)).reshape(heads * rows, 2 * slim)
    halo = lax.ppermute(kv[heads * rows - WINDOW :], "group", [(i, i + 1) for i in range(groups - 1)])
    qg = spread(pack([queries, output_cotangent], [wide, wide], heads)).reshape(heads * rows, 2 * wide)
    od, dkv, back = attention(first, qg, kv, halo)
    more = lax.ppermute(back, "group", [(i + 1, i) for i in range(groups - 1)])
    od = spread(od.reshape(heads, rows, 2 * wide))
    tail = heads * rows - WINDOW
    dkv = jnp.concatenate([dkv[:tail], dkv[tail:] + more.astype(jnp.float32)], 0).astype(jnp.bfloat16)
    dkv = spread(dkv.reshape(heads, rows, 2 * slim))
    attended, grad_queries = unpack(od, [wide, wide])
    key_gradient, value_gradient = unpack(dkv, [slim, slim])
    return attended, grad_queries, key_gradient, value_gradient


def solution(mesh):
    row = 4
    seq, head = mesh.devices.shape
    finer = Mesh(mesh.devices.reshape(seq // row, row, head), ("group", "row", "head"))
    spec = P(("group", "row", "head"), None)
    return jax.shard_map(body, mesh=finer, in_specs=(spec,) * 4, out_specs=(spec,) * 4, check_vma=False)
```

```python
import functools

import jax
import jax.numpy as jnp
from jax import lax
from jax.experimental import pallas as pl
from jax.experimental.pallas import tpu as pltpu
from jax.sharding import Mesh, PartitionSpec as P

D = 128
WINDOW = 1024
BLOCK = 256
CHUNKS = WINDOW // BLOCK
SPAN = WINDOW + BLOCK
SCALE = 168.0 ** (-0.5)
RATE = SCALE * 1.4426950408889634
BF = jnp.bfloat16
F32 = jnp.float32


def cost(flops, bytes_accessed, transcendentals=0):
    return pl.CostEstimate(flops=int(flops), bytes_accessed=int(bytes_accessed), transcendentals=int(transcendentals))


def whole(count):
    return [pl.BlockSpec(memory_space=pltpu.VMEM)] * count


def pack(arrays, widths, heads, step=4):
    rows = arrays[0].shape[0]
    total = sum(widths)

    def kernel(*refs):
        out = refs[-1]
        for j in range(step):
            at = 0
            for ref, w in zip(refs[:-1], widths):
                out[j, :, at : at + w] = ref[:, j * w : (j + 1) * w]
                at += w

    return pl.pallas_call(
        kernel,
        grid=(heads // step,),
        in_specs=[pl.BlockSpec((rows, step * w), lambda i: (0, i)) for w in widths],
        out_specs=pl.BlockSpec((step, rows, total), lambda i: (i, 0, 0)),
        out_shape=jax.ShapeDtypeStruct((heads, rows, total), arrays[0].dtype),
        cost_estimate=cost(0, 4 * heads * rows * total),
        name="pack",
    )(*arrays)


def unpack(packed, widths, step=4):
    heads, rows, total = packed.shape

    def kernel(*refs):
        src = refs[0]
        for j in range(step):
            at = 0
            for ref, w in zip(refs[1:], widths):
                ref[:, j * w : (j + 1) * w] = src[j, :, at : at + w]
                at += w

    return pl.pallas_call(
        kernel,
        grid=(heads // step,),
        in_specs=[pl.BlockSpec((step, rows, total), lambda i: (i, 0, 0))],
        out_specs=[pl.BlockSpec((rows, step * w), lambda i: (0, i)) for w in widths],
        out_shape=[jax.ShapeDtypeStruct((rows, heads * w), packed.dtype) for w in widths],
        cost_estimate=cost(0, 4 * heads * rows * total),
        name="unpack",
    )(packed)


def dot(a, b, ca, cb):
    return lax.dot_general(a, b, (((ca,), (cb,)), ((), ())), preferred_element_type=F32)


def fold(x, op):
    y = x[:, 0:D]
    for i in range(1, BLOCK // D):
        y = op(y, x[:, i * D : (i + 1) * D])
    return y


def attend(q, g, keys, values, old, hide):
    s = dot(q, keys, 1, 1)
    first = jnp.where(old, s[:, 0:BLOCK] if hide is None else s[:, 0:BLOCK] - hide[0], s[:, WINDOW:SPAN])
    parts = [first] + [s[:, c * BLOCK : (c + 1) * BLOCK] for c in range(1, CHUNKS)]
    top = fold(parts[0], jnp.maximum)
    for c in range(1, CHUNKS):
        y = fold(parts[c], jnp.maximum)
        top = jnp.maximum(top, y if hide is None else y - hide[c])
    top = jnp.max(top, axis=-1, keepdims=True) * RATE
    es = [jnp.exp2(parts[0] * RATE - top)]
    for c in range(1, CHUNKS):
        es.append(jnp.exp2(parts[c] * RATE - (top if hide is None else top + hide[c])))
    total = fold(es[0], jnp.add)
    for e in es[1:]:
        total = total + fold(e, jnp.add)
    inv = 1.0 / jnp.sum(total, axis=-1, keepdims=True)
    gf = g.astype(F32)
    gs = (gf * inv).astype(BF)
    eb = [e.astype(BF) for e in es]
    zero = jnp.zeros_like(eb[0])
    eb = jnp.concatenate([jnp.where(old, eb[0], zero)] + eb[1:] + [jnp.where(old, zero, eb[0])], axis=1)
    out = (dot(eb, values, 1, 0) * inv).astype(BF)
    delta = jnp.sum(gf * out.astype(F32), axis=-1, keepdims=True) * inv
    dp = dot(gs, values, 1, 1)
    dparts = [jnp.where(old, dp[:, 0:BLOCK], dp[:, WINDOW:SPAN])]
    dparts += [dp[:, c * BLOCK : (c + 1) * BLOCK] for c in range(1, CHUNKS)]
    ds = [(e * (x - delta)).astype(BF) for e, x in zip(es, dparts)]
    ds = jnp.concatenate([jnp.where(old, ds[0], zero)] + ds[1:] + [jnp.where(old, zero, ds[0])], axis=1)
    dq = (dot(ds, keys, 1, 0) * SCALE).astype(BF)
    return out, dq, (q, ds, gs, eb)


def attend_half(half, factor, qg, ka, a0, kb, b0, hide_when, acc_k, acc_v, put):
    row = lax.broadcasted_iota(jnp.int32, (BLOCK, BLOCK), 0)
    col = lax.broadcasted_iota(jnp.int32, (BLOCK, BLOCK), 1)
    old = col > row
    for b in range(CHUNKS):
        r = b * BLOCK
        rows = slice(half * WINDOW + r, half * WINDOW + r + BLOCK)
        ext = jnp.concatenate([ka[a0 + r : a0 + WINDOW, :], kb[b0 : b0 + r + BLOCK, :]], axis=0)
        keys, values = ext[:, 0:D], ext[:, D : 2 * D]
        hide = None
        if hide_when is not None:
            hide = [jnp.where(hide_when, 1e30, 0.0).astype(F32) if b + c < CHUNKS else 0.0 for c in range(CHUNKS)]
        saved = []
        for h in range(factor):
            q = qg[rows, h * D : (h + 1) * D]
            g = qg[rows, (factor + h) * D : (factor + h + 1) * D]
            out, dq, kept = attend(q, g, keys, values, old, hide)
            put(r, h, out, dq)
            saved.append(kept)
        dk = dot(*[jnp.concatenate([x[i] for x in saved], axis=0) for i in (0, 1)], 0, 0)
        dv = dot(*[jnp.concatenate([x[i] for x in saved], axis=0) for i in (2, 3)], 0, 0)
        seen = 0 if b == 0 else WINDOW
        for acc, part in ((acc_k, dk), (acc_v, dv)):
            if seen:
                acc[:, r : r + seen] += part[:, 0:seen]
            acc[:, r + seen : r + SPAN] = part[:, seen:SPAN]


def first_kernel(factor, lead_ref, qg, kv, halo, od, back, part, acc_k, acc_v):
    def put(r, h, out, dq):
        od[r : r + BLOCK, h * D : (h + 1) * D] = out
        od[r : r + BLOCK, (factor + h) * D : (factor + h + 1) * D] = dq

    attend_half(0, factor, qg, halo, 0, kv, 0, lead_ref[0] == 1, acc_k, acc_v, put)
    back[:, 0:D] = (acc_k[:, 0:WINDOW].T * SCALE).astype(BF)
    back[:, D : 2 * D] = acc_v[:, 0:WINDOW].T.astype(BF)
    part[:, 0:D] = acc_k[:, WINDOW : 2 * WINDOW].T
    part[:, D : 2 * D] = acc_v[:, WINDOW : 2 * WINDOW].T


def second_kernel(factor, qg, kv, od, part, out, last, acc_k, acc_v):
    width = 2 * factor * D
    out[0:WINDOW, 0:width] = od[...]

    def put(r, h, o, dq):
        out[WINDOW + r : WINDOW + r + BLOCK, h * D : (h + 1) * D] = o
        out[WINDOW + r : WINDOW + r + BLOCK, (factor + h) * D : (factor + h + 1) * D] = dq

    attend_half(1, factor, qg, kv, 0, kv, WINDOW, None, acc_k, acc_v, put)
    out[0:WINDOW, width : width + D] = ((acc_k[:, 0:WINDOW].T + part[:, 0:D]) * SCALE).astype(BF)
    out[0:WINDOW, width + D : width + 2 * D] = (acc_v[:, 0:WINDOW].T + part[:, D : 2 * D]).astype(BF)
    last[:, 0:D] = acc_k[:, WINDOW : 2 * WINDOW].T * SCALE
    last[:, D : 2 * D] = acc_v[:, WINDOW : 2 * WINDOW].T


def half_call(kernel, name, factor, out_shape, operands, scalars=0):
    pairs = factor * WINDOW * SPAN
    return pl.pallas_call(
        functools.partial(kernel, factor),
        in_specs=[pl.BlockSpec(memory_space=pltpu.SMEM)] * scalars + whole(len(operands) - scalars),
        out_specs=whole(len(out_shape)),
        out_shape=out_shape,
        scratch_shapes=[pltpu.VMEM((D, 2 * WINDOW), F32)] * 2,
        compiler_params=pltpu.CompilerParams(vmem_limit_bytes=40 * 1024 * 1024),
        cost_estimate=cost(12 * pairs * D, 8e6, pairs),
        name=name,
    )(*operands)


def body(queries, keys, values, output_cotangent):
    axes = ("row", "head")
    heads = lax.axis_size("row") * lax.axis_size("head")
    rows = queries.shape[0]
    wide = queries.shape[1] // heads
    slim = keys.shape[1] // heads
    factor = wide // D
    groups = lax.axis_size("group")
    tokens = heads * rows
    lead = (lax.axis_index("group") == 0).astype(jnp.int32).reshape(1)

    def spread(x):
        return lax.all_to_all(x, axes, split_axis=0, concat_axis=0, tiled=True)

    kv = spread(pack([keys, values], [slim, slim], heads)).reshape(tokens, 2 * slim)
    halo = lax.ppermute(kv[tokens - WINDOW :], "group", [(i, i + 1) for i in range(groups - 1)])
    qg = spread(pack([queries, output_cotangent], [wide, wide], heads)).reshape(tokens, 2 * wide)
    od, back, part = half_call(
        first_kernel,
        "attend_first",
        factor,
        [
            jax.ShapeDtypeStruct((WINDOW, 2 * wide), BF),
            jax.ShapeDtypeStruct((WINDOW, 2 * slim), BF),
            jax.ShapeDtypeStruct((WINDOW, 2 * slim), F32),
        ],
        [lead, qg, kv, halo],
        scalars=1,
    )
    more = lax.ppermute(back, "group", [(i + 1, i) for i in range(groups - 1)])
    out, last = half_call(
        second_kernel,
        "attend_second",
        factor,
        [jax.ShapeDtypeStruct((tokens, 2 * (wide + slim)), BF), jax.ShapeDtypeStruct((WINDOW, 2 * slim), F32)],
        [qg, kv, od, part],
    )
    out = out.at[WINDOW:, 2 * wide :].set((last + more.astype(F32)).astype(BF))
    out = spread(out.reshape(heads, rows, 2 * (wide + slim)))
    return unpack(out, [wide, wide, slim, slim])


def solution(mesh):
    row = 4
    seq, head = mesh.devices.shape
    finer = Mesh(mesh.devices.reshape(seq // row, row, head), ("group", "row", "head"))
    spec = P(("group", "row", "head"), None)
    return jax.shard_map(body, mesh=finer, in_specs=(spec,) * 4, out_specs=(spec,) * 4, check_vma=False)
```

```python
import functools

import jax
import jax.numpy as jnp
from jax import lax
from jax.experimental import pallas as pl
from jax.experimental.pallas import tpu as pltpu
from jax.sharding import Mesh, PartitionSpec as P


D = 128
WINDOW = 1024
BLOCK = 256
CHUNKS = WINDOW // BLOCK
SPAN = WINDOW + BLOCK
SCALE = 168.0 ** (-0.5)
RATE = SCALE * 1.4426950408889634
BF = jnp.bfloat16
F32 = jnp.float32


def cost(flops, bytes_accessed, transcendentals=0):
    return pl.CostEstimate(flops=int(flops), bytes_accessed=int(bytes_accessed), transcendentals=int(transcendentals))


def whole(count):
    return [pl.BlockSpec(memory_space=pltpu.VMEM)] * count


PIECES = 4


def strips(widths, heads):
    for j in range(heads):
        at = 0
        for i, w in enumerate(widths):
            yield j, i, j * w, at, w
            at += w


def pack(arrays, widths, heads):
    rows, total, n = arrays[0].shape[0], sum(widths), len(widths)

    def kernel(*refs):
        src, out, held, sems = refs[:n], refs[n], refs[n + 1 : -1], refs[-1]
        copies = []
        for p in range(PIECES):
            for i, w in enumerate(widths):
                cols = pl.ds(p * w * heads // PIECES, w * heads // PIECES)
                copies.append(pltpu.make_async_copy(src[i].at[:, cols], held[i].at[:, cols], sems.at[p * n + i]))
        for copy in copies:
            copy.start()
        for j, i, there, here, w in strips(widths, heads):
            if j % (heads // PIECES) == 0:
                copies[j // (heads // PIECES) * n + i].wait()
            out[j, :, here : here + w] = held[i][:, there : there + w]

    return pl.pallas_call(
        kernel,
        in_specs=[pl.BlockSpec(memory_space=pltpu.HBM)] * n,
        out_specs=pl.BlockSpec(memory_space=pltpu.VMEM),
        out_shape=jax.ShapeDtypeStruct((heads, rows, total), arrays[0].dtype),
        scratch_shapes=[pltpu.VMEM(x.shape, x.dtype) for x in arrays] + [pltpu.SemaphoreType.DMA((PIECES * n,))],
        cost_estimate=cost(0, 4 * heads * rows * total),
        name="pack",
    )(*arrays)


def unpack(packed, widths):
    heads, rows, total = packed.shape
    n = len(widths)
    shapes = [jax.ShapeDtypeStruct((rows, heads * w), packed.dtype) for w in widths]

    def kernel(*refs):
        src, out, held, sems = refs[0], refs[1 : 1 + n], refs[1 + n : -1], refs[-1]
        copies = []
        for j, i, there, here, w in strips(widths, heads):
            held[i][:, there : there + w] = src[j, :, here : here + w]
            p, last = divmod(j + 1, heads // PIECES)
            if last == 0:
                cols = pl.ds((p - 1) * w * heads // PIECES, w * heads // PIECES)
                copy = pltpu.make_async_copy(held[i].at[:, cols], out[i].at[:, cols], sems.at[(p - 1) * n + i])
                copy.start()
                copies.append(copy)
        for copy in copies:
            copy.wait()

    return pl.pallas_call(
        kernel,
        in_specs=[pl.BlockSpec(memory_space=pltpu.VMEM)],
        out_specs=[pl.BlockSpec(memory_space=pl.ANY)] * n,
        out_shape=shapes,
        scratch_shapes=[pltpu.VMEM(x.shape, x.dtype) for x in shapes] + [pltpu.SemaphoreType.DMA((PIECES * n,))],
        compiler_params=pltpu.CompilerParams(vmem_limit_bytes=16 * 1024 * 1024),
        cost_estimate=cost(0, 4 * heads * rows * total),
        name="unpack",
    )(packed)


def dot(a, b, ca, cb):
    return lax.dot_general(a, b, (((ca,), (cb,)), ((), ())), preferred_element_type=F32)


def fold(x, op):
    y = x[:, 0:D]
    for i in range(1, BLOCK // D):
        y = op(y, x[:, i * D : (i + 1) * D])
    return y


def attend(q, g, keys, values, old, hide):
    s = dot(q, keys, 1, 1)
    first = jnp.where(old, s[:, 0:BLOCK] if hide is None else s[:, 0:BLOCK] - hide[0], s[:, WINDOW:SPAN])
    parts = [first] + [s[:, c * BLOCK : (c + 1) * BLOCK] for c in range(1, CHUNKS)]
    top = fold(parts[0], jnp.maximum)
    for c in range(1, CHUNKS):
        y = fold(parts[c], jnp.maximum)
        top = jnp.maximum(top, y if hide is None else y - hide[c])
    top = jnp.max(top, axis=-1, keepdims=True) * RATE
    es = [jnp.exp2(parts[0] * RATE - top)]
    for c in range(1, CHUNKS):
        es.append(jnp.exp2(parts[c] * RATE - (top if hide is None else top + hide[c])))
    total = fold(es[0], jnp.add)
    for e in es[1:]:
        total = total + fold(e, jnp.add)
    inv = 1.0 / jnp.sum(total, axis=-1, keepdims=True)
    gf = g.astype(F32)
    gs = (gf * inv).astype(BF)
    eb = [e.astype(BF) for e in es]
    zero = jnp.zeros_like(eb[0])
    eb = jnp.concatenate([jnp.where(old, eb[0], zero)] + eb[1:] + [jnp.where(old, zero, eb[0])], axis=1)
    out = (dot(eb, values, 1, 0) * inv).astype(BF)
    delta = jnp.sum(gf * out.astype(F32), axis=-1, keepdims=True) * inv
    dp = dot(gs, values, 1, 1)
    dparts = [jnp.where(old, dp[:, 0:BLOCK], dp[:, WINDOW:SPAN])]
    dparts += [dp[:, c * BLOCK : (c + 1) * BLOCK] for c in range(1, CHUNKS)]
    ds = [(e * (x - delta)).astype(BF) for e, x in zip(es, dparts)]
    ds = jnp.concatenate([jnp.where(old, ds[0], zero)] + ds[1:] + [jnp.where(old, zero, ds[0])], axis=1)
    dq = (dot(ds, keys, 1, 0) * SCALE).astype(BF)
    return out, dq, (q, ds, gs, eb)


def attend_half(half, factor, qg, ka, a0, kb, b0, hide_when, acc_k, acc_v, put):
    row = lax.broadcasted_iota(jnp.int32, (BLOCK, BLOCK), 0)
    col = lax.broadcasted_iota(jnp.int32, (BLOCK, BLOCK), 1)
    old = col > row
    for b in range(CHUNKS):
        r = b * BLOCK
        rows = slice(half * WINDOW + r, half * WINDOW + r + BLOCK)
        ext = jnp.concatenate([ka[a0 + r : a0 + WINDOW, :], kb[b0 : b0 + r + BLOCK, :]], axis=0)
        keys, values = ext[:, 0:D], ext[:, D : 2 * D]
        hide = None
        if hide_when is not None:
            hide = [jnp.where(hide_when, 1e30, 0.0).astype(F32) if b + c < CHUNKS else 0.0 for c in range(CHUNKS)]
        saved = []
        for h in range(factor):
            q = qg[rows, h * D : (h + 1) * D]
            g = qg[rows, (factor + h) * D : (factor + h + 1) * D]
            out, dq, kept = attend(q, g, keys, values, old, hide)
            put(r, h, out, dq)
            saved.append(kept)
        dk = dot(*[jnp.concatenate([x[i] for x in saved], axis=0) for i in (0, 1)], 0, 0)
        dv = dot(*[jnp.concatenate([x[i] for x in saved], axis=0) for i in (2, 3)], 0, 0)
        seen = 0 if b == 0 else WINDOW
        for acc, part in ((acc_k, dk), (acc_v, dv)):
            if seen:
                acc[:, r : r + seen] += part[:, 0:seen]
            acc[:, r + seen : r + SPAN] = part[:, seen:SPAN]


def first_kernel(factor, lead_ref, data, halo, od, back, part, acc_k, acc_v):
    def put(r, h, out, dq):
        od[r : r + BLOCK, h * D : (h + 1) * D] = out
        od[r : r + BLOCK, (factor + h) * D : (factor + h + 1) * D] = dq

    kv = data.at[:, 2 * factor * D :]
    attend_half(0, factor, data, halo, 0, kv, 0, lead_ref[0] == 1, acc_k, acc_v, put)
    back[:, 0:D] = (acc_k[:, 0:WINDOW].T * SCALE).astype(BF)
    back[:, D : 2 * D] = acc_v[:, 0:WINDOW].T.astype(BF)
    part[:, 0:D] = acc_k[:, WINDOW : 2 * WINDOW].T
    part[:, D : 2 * D] = acc_v[:, WINDOW : 2 * WINDOW].T


def second_kernel(factor, data, od, part, out, last, acc_k, acc_v):
    width = 2 * factor * D
    out[0:WINDOW, 0:width] = od[...]

    def put(r, h, o, dq):
        out[WINDOW + r : WINDOW + r + BLOCK, h * D : (h + 1) * D] = o
        out[WINDOW + r : WINDOW + r + BLOCK, (factor + h) * D : (factor + h + 1) * D] = dq

    kv = data.at[:, 2 * factor * D :]
    attend_half(1, factor, data, kv, 0, kv, WINDOW, None, acc_k, acc_v, put)
    out[0:WINDOW, width : width + D] = ((acc_k[:, 0:WINDOW].T + part[:, 0:D]) * SCALE).astype(BF)
    out[0:WINDOW, width + D : width + 2 * D] = (acc_v[:, 0:WINDOW].T + part[:, D : 2 * D]).astype(BF)
    last[:, 0:D] = acc_k[:, WINDOW : 2 * WINDOW].T * SCALE
    last[:, D : 2 * D] = acc_v[:, WINDOW : 2 * WINDOW].T


def half_call(kernel, factor, out_shape, operands, scalars=0):
    pairs = factor * WINDOW * SPAN
    return pl.pallas_call(
        functools.partial(kernel, factor),
        in_specs=[pl.BlockSpec(memory_space=pltpu.SMEM)] * scalars + whole(len(operands) - scalars),
        out_specs=whole(len(out_shape)),
        out_shape=out_shape,
        scratch_shapes=[pltpu.VMEM((D, 2 * WINDOW), F32)] * 2,
        compiler_params=pltpu.CompilerParams(vmem_limit_bytes=20 * 1024 * 1024),
        cost_estimate=cost(12 * pairs * D, 8e6, pairs),
    )(*operands)


def body(queries, keys, values, output_cotangent):
    axes = ("row", "head")
    heads = lax.axis_size("row") * lax.axis_size("head")
    rows = queries.shape[0]
    wide = queries.shape[1] // heads
    slim = keys.shape[1] // heads
    factor = wide // D
    groups = lax.axis_size("group")
    tokens = heads * rows
    lead = (lax.axis_index("group") == 0).astype(jnp.int32).reshape(1)

    def spread(x):
        return lax.all_to_all(x, axes, split_axis=0, concat_axis=0, tiled=True)

    packed = pack([queries, output_cotangent, keys, values], [wide, wide, slim, slim], heads)
    data = spread(packed).reshape(tokens, 2 * (wide + slim))
    halo = lax.ppermute(data[tokens - WINDOW :, 2 * wide :], "group", [(i, i + 1) for i in range(groups - 1)])
    od, back, part = half_call(
        first_kernel,
        factor,
        [
            jax.ShapeDtypeStruct((WINDOW, 2 * wide), BF),
            jax.ShapeDtypeStruct((WINDOW, 2 * slim), BF),
            jax.ShapeDtypeStruct((WINDOW, 2 * slim), F32),
        ],
        [lead, data, halo],
        scalars=1,
    )
    more = lax.ppermute(back, "group", [(i + 1, i) for i in range(groups - 1)])
    out, last = half_call(
        second_kernel,
        factor,
        [jax.ShapeDtypeStruct((tokens, 2 * (wide + slim)), BF), jax.ShapeDtypeStruct((WINDOW, 2 * slim), F32)],
        [data, od, part],
    )
    out = out.at[WINDOW:, 2 * wide :].set((last + more.astype(F32)).astype(BF))
    out = spread(out.reshape(heads, rows, 2 * (wide + slim)))
    return unpack(out, [wide, wide, slim, slim])


def solution(mesh):
    row = 4
    seq, head = mesh.devices.shape
    finer = Mesh(mesh.devices.reshape(seq // row, row, head), ("group", "row", "head"))
    spec = P(("group", "row", "head"), None)
    return jax.shard_map(body, mesh=finer, in_specs=(spec,) * 4, out_specs=(spec,) * 4, check_vma=False)
```

```python
import jax
import jax.numpy as jnp
from jax import lax
from jax.experimental import pallas as pl
from jax.experimental.pallas import tpu as pltpu
from jax.sharding import Mesh, PartitionSpec as P


D = 128
WINDOW = 1024
BLOCK = 256
CHUNKS = WINDOW // BLOCK
SPAN = WINDOW + BLOCK
SCALE = 168.0 ** (-0.5)
RATE = SCALE * 1.4426950408889634
BF = jnp.bfloat16
F32 = jnp.float32


def cost(flops, bytes_accessed, transcendentals=0):
    return pl.CostEstimate(flops=int(flops), bytes_accessed=int(bytes_accessed), transcendentals=int(transcendentals))


VMEM = pl.BlockSpec(memory_space=pltpu.VMEM)
SMEM = pl.BlockSpec(memory_space=pltpu.SMEM)
AWAY = pl.BlockSpec(memory_space=pl.ANY)
SUMS = (2, D, 2 * WINDOW)


PIECES = 4


def strips(cuts, heads):
    for j in range(heads):
        at = 0
        for i, per, start, w in cuts:
            yield j, i, j * per + start, at, w
            at += w


def pack(arrays, cuts, heads):
    rows, total, n = arrays[0].shape[0], sum(cut[3] for cut in cuts), len(arrays)

    def kernel(*refs):
        src, out, held, made, sems = refs[:n], refs[n], refs[n + 1 : -2], refs[-2], refs[-1]
        copies = []
        for p in range(PIECES):
            for i in range(n):
                w = arrays[i].shape[1] // PIECES
                copies.append(pltpu.make_async_copy(src[i].at[:, pl.ds(p * w, w)], held[i].at[:, pl.ds(p * w, w)], sems.at[p * n + i]))
        for copy in copies:
            copy.start()
        outs = []
        some = heads // PIECES
        for p in range(PIECES):
            for copy in copies[p * n : (p + 1) * n]:
                copy.wait()
            for j, i, there, here, w in strips(cuts, heads):
                if j // some == p:
                    made[j, :, here : here + w] = held[i][:, there : there + w]
            outs.append(pltpu.make_async_copy(made.at[pl.ds(p * some, some)], out.at[pl.ds(p * some, some)], sems.at[PIECES * n + p]))
            outs[-1].start()
        for copy in outs:
            copy.wait()

    return pl.pallas_call(
        kernel,
        in_specs=[AWAY] * n,
        out_specs=AWAY,
        out_shape=pltpu.HBM((heads, rows, total), arrays[0].dtype),
        scratch_shapes=[pltpu.VMEM(x.shape, x.dtype) for x in arrays]
        + [pltpu.VMEM((heads, rows, total), arrays[0].dtype), pltpu.SemaphoreType.DMA((PIECES * (n + 1),))],
        compiler_params=pltpu.CompilerParams(vmem_limit_bytes=20 * 1024 * 1024),
        cost_estimate=cost(0, 4 * heads * rows * total),
        name="pack",
    )(*[pltpu.with_memory_space_constraint(x, pltpu.HBM) for x in arrays])


def unpack(chunks, cuts, columns):
    heads, rows, _ = chunks[0].shape
    m, n = len(chunks), len(columns)
    shapes = [jax.ShapeDtypeStruct((rows, heads * w), chunks[0].dtype) for w in columns]

    def kernel(*refs):
        src, out, held, sems = refs[:m], refs[m : m + n], refs[m + n : -1], refs[-1]
        copies = []
        for p in range(PIECES):
            for c in range(m):
                for j, i, there, here, w in strips(cuts[c], heads):
                    if j * PIECES // heads == p:
                        held[i][:, there : there + w] = src[c][j, :, here : here + w]
            for i in range(n):
                w = shapes[i].shape[1] // PIECES
                copies.append(pltpu.make_async_copy(held[i].at[:, pl.ds(p * w, w)], out[i].at[:, pl.ds(p * w, w)], sems.at[p * n + i]))
                copies[-1].start()
        for copy in copies:
            copy.wait()

    return pl.pallas_call(
        kernel,
        in_specs=[VMEM] * m,
        out_specs=[AWAY] * n,
        out_shape=shapes,
        scratch_shapes=[pltpu.VMEM(x.shape, x.dtype) for x in shapes]
        + [pltpu.SemaphoreType.DMA((PIECES * n,))],
        compiler_params=pltpu.CompilerParams(vmem_limit_bytes=16 * 1024 * 1024),
        cost_estimate=cost(0, 4 * sum(x.size for x in chunks)),
        name="unpack",
    )(*chunks)


def stage(x):
    def kernel(src, out, sem):
        copy = pltpu.make_async_copy(src, out, sem.at[0])
        copy.start()
        copy.wait()

    return pl.pallas_call(
        kernel,
        in_specs=[AWAY],
        out_specs=VMEM,
        out_shape=jax.ShapeDtypeStruct(x.shape, x.dtype),
        scratch_shapes=[pltpu.SemaphoreType.DMA((1,))],
        compiler_params=pltpu.CompilerParams(vmem_limit_bytes=20 * 1024 * 1024),
        cost_estimate=cost(0, 4 * x.size),
        name="stage",
    )(pltpu.with_memory_space_constraint(x, pltpu.HBM))


def dot(a, b, ca, cb):
    return lax.dot_general(a, b, (((ca,), (cb,)), ((), ())), preferred_element_type=F32)


def fold(x, op):
    y = x[:, 0:D]
    for i in range(1, BLOCK // D):
        y = op(y, x[:, i * D : (i + 1) * D])
    return y


def attend(q, read_g, keys, values, old, hide):
    s = dot(q, keys, 1, 1)
    first = jnp.where(old, s[:, 0:BLOCK] if hide is None else s[:, 0:BLOCK] - hide[0], s[:, WINDOW:SPAN])
    parts = [first] + [s[:, c * BLOCK : (c + 1) * BLOCK] for c in range(1, CHUNKS)]
    top = fold(parts[0], jnp.maximum)
    for c in range(1, CHUNKS):
        y = fold(parts[c], jnp.maximum)
        top = jnp.maximum(top, y if hide is None else y - hide[c])
    top = jnp.max(top, axis=-1, keepdims=True) * RATE
    es = [jnp.exp2(parts[0] * RATE - top)]
    for c in range(1, CHUNKS):
        es.append(jnp.exp2(parts[c] * RATE - (top if hide is None else top + hide[c])))
    total = fold(es[0], jnp.add)
    for e in es[1:]:
        total = total + fold(e, jnp.add)
    inv = 1.0 / jnp.sum(total, axis=-1, keepdims=True)
    gf = read_g().astype(F32)
    gs = (gf * inv).astype(BF)
    eb = [e.astype(BF) for e in es]
    zero = jnp.zeros_like(eb[0])
    eb = jnp.concatenate([jnp.where(old, eb[0], zero)] + eb[1:] + [jnp.where(old, zero, eb[0])], axis=1)
    out = (dot(eb, values, 1, 0) * inv).astype(BF)
    delta = jnp.sum(gf * out.astype(F32), axis=-1, keepdims=True) * inv
    dp = dot(gs, values, 1, 1)
    dparts = [jnp.where(old, dp[:, 0:BLOCK], dp[:, WINDOW:SPAN])]
    dparts += [dp[:, c * BLOCK : (c + 1) * BLOCK] for c in range(1, CHUNKS)]
    ds = [(e * (x - delta)).astype(BF) for e, x in zip(es, dparts)]
    ds = jnp.concatenate([jnp.where(old, ds[0], zero)] + ds[1:] + [jnp.where(old, zero, ds[0])], axis=1)
    dq = (dot(ds, keys, 1, 0) * SCALE).astype(BF)
    return out, dq, (q, ds, gs, eb)


def attend_half(qs, row0, gs, g0, ka, a0, kb, b0, hide_when, acc, put, done, arrive=None):
    row = lax.broadcasted_iota(jnp.int32, (BLOCK, BLOCK), 0)
    col = lax.broadcasted_iota(jnp.int32, (BLOCK, BLOCK), 1)
    old = col > row
    for b in range(CHUNKS):
        r = b * BLOCK
        keys = jnp.concatenate([ka[a0 + r : a0 + WINDOW, 0:D], kb[b0 : b0 + r + BLOCK, 0:D]], axis=0)
        values = jnp.concatenate([ka[a0 + r : a0 + WINDOW, D : 2 * D], kb[b0 : b0 + r + BLOCK, D : 2 * D]], axis=0)
        hide = None
        if hide_when is not None:
            hide = [jnp.where(hide_when, 1e30, 0.0).astype(F32) if b + c < CHUNKS else 0.0 for c in range(CHUNKS)]
        q = qs[row0 + r : row0 + r + BLOCK, :]

        def read_g():
            if r == 0 and arrive is not None:
                arrive.wait()
            return gs[g0 + r : g0 + r + BLOCK, :]

        out, dq, (q, ds, g, eb) = attend(q, read_g, keys, values, old, hide)
        put(r, out, dq)
        seen = 0 if b == 0 else WINDOW
        for i, part in enumerate((dot(q, ds, 0, 0), dot(g, eb, 0, 0))):
            if seen:
                acc[i, :, r : r + seen] += part[:, 0:seen]
            acc[i, :, r + seen : r + SPAN] = part[:, seen:SPAN]
        if done is not None:
            done(r)


def store_rows(ref, row0):
    def put(r, out, dq):
        ref[row0 + r : row0 + r + BLOCK, 0:D] = out
        ref[row0 + r : row0 + r + BLOCK, D : 2 * D] = dq

    return put


def sender(rows, od, row0, acc, sums, sems):
    copies = []

    def send(src, dst):
        copies.append(pltpu.make_async_copy(src, dst, sems.at[len(copies)]))
        copies[-1].start()

    def done(r):
        if r < WINDOW - 2 * BLOCK:
            return
        for r in range(0, r + BLOCK, BLOCK) if r + BLOCK < WINDOW else [r]:
            ship(r)

    def ship(r):
        send(rows.at[pl.ds(r, BLOCK)], od.at[pl.ds(row0 + r, BLOCK), pl.ds(0, 2 * D)])
        if sums is not None:
            cols = pl.ds(r, BLOCK if r + BLOCK < WINDOW else SPAN)
            send(acc.at[:, :, cols], sums.at[:, :, cols])

    return copies, done


def wait_all(copies):
    for copy in copies:
        copy.wait()


LOW, HIGH = slice(0, WINDOW), slice(WINDOW, 2 * WINDOW)
LOW_COLS, HIGH_COLS = pl.ds(0, WINDOW), pl.ds(WINDOW, WINDOW)
GRADS = pl.ds(2 * D, 2 * D)
SCALES = (SCALE, 1.0)


def second_of_first_head(data, od, sums, acc, rows, sems):
    copies, done = sender(rows, od, WINDOW, acc, sums, sems)
    attend_half(data.at[:, 2 * D : 3 * D], WINDOW, data.at[:, 3 * D : 4 * D], WINDOW, data, 0, data, WINDOW, None, acc, store_rows(rows, 0), done)
    wait_all(copies)


def first_of_first_head(lead, data, halo, _, od, sums, acc, rows, sems):
    copies, done = sender(rows, od, 0, acc, sums, sems)
    attend_half(data.at[:, 2 * D : 3 * D], 0, data.at[:, 3 * D : 4 * D], 0, halo, 0, data, 0, lead[0] == 1, acc, store_rows(rows, 0), done)
    wait_all(copies)


def first_of_second_head(lead, data, last_g, halo, before, out, back, own, acc, rows, sums, cotangents, sems):
    load = pltpu.make_async_copy(before.at[:, :, LOW_COLS], sums, sems.at[CHUNKS])
    load.start()
    copies, done = sender(rows, out, 0, acc, None, sems)
    arrive = pltpu.make_async_copy(last_g.at[LOW_COLS], cotangents, sems.at[2 * CHUNKS])
    arrive.start()
    attend_half(data.at[:, 4 * D : 5 * D], 0, cotangents, 0, halo, 0, data, 0, lead[0] == 1, acc, store_rows(rows, 0), done, arrive)
    copies.append(pltpu.make_async_copy(acc.at[:, :, HIGH_COLS], own, sems.at[CHUNKS + 1]))
    copies[-1].start()
    load.wait()
    for i in range(2):
        back[i] = ((acc[i, :, LOW] + sums[i]) * SCALES[i]).astype(BF)
    wait_all(copies)


def second_of_second_head(data, last_g, _, sums_s0, sums_f0, sums_f1, out, last, acc, rows, sums, more, most, grads, cotangents, sems):
    loads = [
        pltpu.make_async_copy(sums_s0, sums, sems.at[CHUNKS]),
        pltpu.make_async_copy(sums_f0.at[:, :, HIGH_COLS], more, sems.at[CHUNKS + 1]),
        pltpu.make_async_copy(sums_f1, most, sems.at[CHUNKS + 2]),
    ]
    for load in loads:
        load.start()
    copies, done = sender(rows, out, WINDOW, acc, None, sems)
    arrive = pltpu.make_async_copy(last_g.at[HIGH_COLS], cotangents, sems.at[2 * CHUNKS])
    arrive.start()
    attend_half(data.at[:, 4 * D : 5 * D], WINDOW, cotangents, 0, data, 0, data, WINDOW, None, acc, store_rows(rows, 0), done, arrive)
    wait_all(loads)
    for i in range(2):
        total = (acc[i, :, LOW] + sums[i, :, LOW]) + (more[i] + most[i])
        grads[:, i * D : (i + 1) * D] = (total.T * SCALES[i]).astype(BF)
    copies.append(pltpu.make_async_copy(grads, out.at[LOW_COLS, GRADS], sems.at[CHUNKS + 3]))
    copies[-1].start()
    for i in range(2):
        last[i] = (acc[i, :, HIGH] + sums[i, :, HIGH]) * SCALES[i]
    wait_all(copies)


def join_gradients(last, more, _, out, grads, sem):
    for i in range(2):
        grads[:, i * D : (i + 1) * D] = (last[i] + more[i].astype(F32)).T.astype(BF)
    copy = pltpu.make_async_copy(grads, out.at[HIGH_COLS, GRADS], sem.at[0])
    copy.start()
    copy.wait()


def call(kernel, operands, in_specs, outs, out_specs, scratch, aliases=None):
    pairs = WINDOW * SPAN
    operands = [pltpu.with_memory_space_constraint(x, pltpu.HBM) if spec is AWAY else x for x, spec in zip(operands, in_specs)]
    return pl.pallas_call(
        kernel,
        in_specs=in_specs,
        out_specs=out_specs,
        out_shape=[pltpu.HBM(*out) if spec is AWAY else jax.ShapeDtypeStruct(*out) for out, spec in zip(outs, out_specs)],
        scratch_shapes=[pltpu.VMEM(SUMS, F32)] + scratch + [pltpu.SemaphoreType.DMA((2 * CHUNKS + 1,))],
        input_output_aliases=aliases or {},
        compiler_params=pltpu.CompilerParams(vmem_limit_bytes=20 * 1024 * 1024),
        cost_estimate=cost(12 * pairs * D, 8e6, pairs),
    )(*operands)


def body(queries, keys, values, output_cotangent):
    axes = ("row", "head")
    heads = lax.axis_size("row") * lax.axis_size("head")
    rows = queries.shape[0]
    groups = lax.axis_size("group")
    tokens = heads * rows
    lead = (lax.axis_index("group") == 0).astype(jnp.int32).reshape(1)

    def spread(x):
        return lax.all_to_all(x, axes, split_axis=0, concat_axis=0, tiled=True)

    part = (2, D, WINDOW)
    sums = (SUMS, F32)
    hold = pltpu.VMEM((WINDOW, 2 * D), BF)
    cotangents = pltpu.VMEM((WINDOW, D), BF)
    first_cuts = [(0, D, 0, D), (1, D, 0, D), (2, 2 * D, 0, D), (3, 2 * D, 0, D), (2, 2 * D, D, D)]
    packed_a = pack([keys, values, queries, output_cotangent], first_cuts, heads)
    packed_b = pack([output_cotangent], [(0, 2 * D, D, D)], heads)
    data = spread(packed_a).reshape(tokens, 5 * D)
    halo = lax.ppermute(data[tokens - WINDOW :, 0 : 2 * D], "group", [(i, i + 1) for i in range(groups - 1)])
    halo = pltpu.with_memory_space_constraint(halo, pltpu.VMEM)
    last_g = spread(packed_b).reshape(tokens, D)
    od_0, sums_s0 = call(second_of_first_head, [data], [VMEM], [((tokens, 2 * D), BF), sums], [AWAY, AWAY], [hold])
    od_0, sums_f0 = call(
        first_of_first_head,
        [lead, data, halo, od_0],
        [SMEM, VMEM, VMEM, AWAY],
        [((tokens, 2 * D), BF), sums],
        [AWAY, AWAY],
        [hold],
        {3: 0},
    )
    out, back, own = call(
        first_of_second_head,
        [lead, data, last_g, halo, sums_f0],
        [SMEM, VMEM, AWAY, VMEM, AWAY],
        [((tokens, 4 * D), BF), (part, BF), (part, F32)],
        [AWAY, VMEM, AWAY],
        [hold, pltpu.VMEM(part, F32), cotangents],
    )
    more = lax.ppermute(back, "group", [(i + 1, i) for i in range(groups - 1)])
    chunks_a = spread(od_0.reshape(heads, rows, 2 * D))
    out, last = call(
        second_of_second_head,
        [data, last_g, out, sums_s0, sums_f0, own],
        [VMEM, AWAY, AWAY, AWAY, AWAY, AWAY],
        [((tokens, 4 * D), BF), (part, F32)],
        [AWAY, VMEM],
        [hold, pltpu.VMEM(SUMS, F32), pltpu.VMEM(part, F32), pltpu.VMEM(part, F32), hold, cotangents],
        {2: 0},
    )
    out = pl.pallas_call(
        join_gradients,
        in_specs=[VMEM, VMEM, AWAY],
        out_specs=AWAY,
        out_shape=pltpu.HBM(out.shape, BF),
        scratch_shapes=[hold, pltpu.SemaphoreType.DMA((1,))],
        input_output_aliases={2: 0},
        compiler_params=pltpu.CompilerParams(vmem_limit_bytes=20 * 1024 * 1024),
        cost_estimate=cost(0, 4e6),
        name="join_gradients",
    )(last, more, pltpu.with_memory_space_constraint(out, pltpu.HBM))
    chunks_b = spread(out.reshape(heads, rows, 4 * D))
    chunks_a = stage(chunks_a)
    return unpack(
        [chunks_a, chunks_b],
        [[(0, 2 * D, 0, D), (1, 2 * D, 0, D)], [(0, 2 * D, D, D), (1, 2 * D, D, D), (2, D, 0, D), (3, D, 0, D)]],
        [2 * D, 2 * D, D, D],
    )


def solution(mesh):
    row = 4
    seq, head = mesh.devices.shape
    finer = Mesh(mesh.devices.reshape(seq // row, row, head), ("group", "row", "head"))
    spec = P(("group", "row", "head"), None)
    return jax.shard_map(body, mesh=finer, in_specs=(spec,) * 4, out_specs=(spec,) * 4, check_vma=False)
```

```python
import jax
import jax.numpy as jnp
from jax import lax
from jax.experimental import pallas as pl
from jax.experimental.pallas import tpu as pltpu
from jax.sharding import Mesh, PartitionSpec as P


D = 128
WINDOW = 1024
BLOCK = 256
CHUNKS = WINDOW // BLOCK
SPAN = WINDOW + BLOCK
SCALE = 168.0 ** (-0.5)
RATE = SCALE * 1.4426950408889634
BF = jnp.bfloat16
F32 = jnp.float32


def cost(flops, bytes_accessed, transcendentals=0):
    return pl.CostEstimate(flops=int(flops), bytes_accessed=int(bytes_accessed), transcendentals=int(transcendentals))


VMEM = pl.BlockSpec(memory_space=pltpu.VMEM)
SMEM = pl.BlockSpec(memory_space=pltpu.SMEM)
AWAY = pl.BlockSpec(memory_space=pl.ANY)
SUMS = (2, D, 2 * WINDOW)


PIECES = 2


def strips(cuts, heads):
    for j in range(heads):
        at = 0
        for i, per, start, w in cuts:
            yield j, i, j * per + start, at, w
            at += w


def pack(arrays, cuts, heads):
    rows, total, n = arrays[0].shape[0], sum(cut[3] for cut in cuts), len(arrays)

    def kernel(*refs):
        src, out, held, made, sems = refs[:n], refs[n], refs[n + 1 : -2], refs[-2], refs[-1]
        copies = []
        for p in range(PIECES):
            for i in range(n):
                w = arrays[i].shape[1] // PIECES
                copies.append(pltpu.make_async_copy(src[i].at[:, pl.ds(p * w, w)], held[i].at[:, pl.ds(p * w, w)], sems.at[p * n + i]))
        for copy in copies:
            copy.start()
        outs = []
        some = heads // PIECES
        for p in range(PIECES):
            for copy in copies[p * n : (p + 1) * n]:
                copy.wait()
            for j, i, there, here, w in strips(cuts, heads):
                if j // some == p:
                    made[j, :, here : here + w] = held[i][:, there : there + w]
            outs.append(pltpu.make_async_copy(made.at[pl.ds(p * some, some)], out.at[pl.ds(p * some, some)], sems.at[PIECES * n + p]))
            outs[-1].start()
        for copy in outs:
            copy.wait()

    return pl.pallas_call(
        kernel,
        in_specs=[AWAY] * n,
        out_specs=AWAY,
        out_shape=pltpu.HBM((heads, rows, total), arrays[0].dtype),
        scratch_shapes=[pltpu.VMEM(x.shape, x.dtype) for x in arrays]
        + [pltpu.VMEM((heads, rows, total), arrays[0].dtype), pltpu.SemaphoreType.DMA((PIECES * (n + 1),))],
        compiler_params=pltpu.CompilerParams(vmem_limit_bytes=20 * 1024 * 1024),
        cost_estimate=cost(0, 4 * heads * rows * total),
        name="pack",
    )(*[pltpu.with_memory_space_constraint(x, pltpu.HBM) for x in arrays])


def unpack(chunks, cuts, columns):
    heads, rows, _ = chunks[0].shape
    m, n = len(chunks), len(columns)
    shapes = [jax.ShapeDtypeStruct((rows, heads * w), chunks[0].dtype) for w in columns]

    def kernel(*refs):
        src, out, held, sems = refs[:m], refs[m : m + n], refs[m + n : -1], refs[-1]
        copies = []
        for p in range(PIECES):
            for c in range(m):
                for j, i, there, here, w in strips(cuts[c], heads):
                    if j * PIECES // heads == p:
                        held[i][:, there : there + w] = src[c][j, :, here : here + w]
            for i in range(n):
                w = shapes[i].shape[1] // PIECES
                copies.append(pltpu.make_async_copy(held[i].at[:, pl.ds(p * w, w)], out[i].at[:, pl.ds(p * w, w)], sems.at[p * n + i]))
                copies[-1].start()
        for copy in copies:
            copy.wait()

    return pl.pallas_call(
        kernel,
        in_specs=[VMEM] * m,
        out_specs=[AWAY] * n,
        out_shape=shapes,
        scratch_shapes=[pltpu.VMEM(x.shape, x.dtype) for x in shapes]
        + [pltpu.SemaphoreType.DMA((PIECES * n,))],
        compiler_params=pltpu.CompilerParams(vmem_limit_bytes=16 * 1024 * 1024),
        cost_estimate=cost(0, 4 * sum(x.size for x in chunks)),
        name="unpack",
    )(*chunks)


def stage(x):
    def kernel(src, out, sem):
        copy = pltpu.make_async_copy(src, out, sem.at[0])
        copy.start()
        copy.wait()

    return pl.pallas_call(
        kernel,
        in_specs=[AWAY],
        out_specs=VMEM,
        out_shape=jax.ShapeDtypeStruct(x.shape, x.dtype),
        scratch_shapes=[pltpu.SemaphoreType.DMA((1,))],
        compiler_params=pltpu.CompilerParams(vmem_limit_bytes=20 * 1024 * 1024),
        cost_estimate=cost(0, 4 * x.size),
        name="stage",
    )(pltpu.with_memory_space_constraint(x, pltpu.HBM))


def dot(a, b, ca, cb):
    return lax.dot_general(a, b, (((ca,), (cb,)), ((), ())), preferred_element_type=F32)


def fold(x, op):
    y = x[:, 0:D]
    for i in range(1, BLOCK // D):
        y = op(y, x[:, i * D : (i + 1) * D])
    return y


def attend(q, g, keys, values, old, hide):
    s = dot(q, keys, 1, 1)
    first = jnp.where(old, s[:, 0:BLOCK] if hide is None else s[:, 0:BLOCK] - hide[0], s[:, WINDOW:SPAN])
    parts = [first] + [s[:, c * BLOCK : (c + 1) * BLOCK] for c in range(1, CHUNKS)]
    top = fold(parts[0], jnp.maximum)
    for c in range(1, CHUNKS):
        y = fold(parts[c], jnp.maximum)
        top = jnp.maximum(top, y if hide is None else y - hide[c])
    top = jnp.max(top, axis=-1, keepdims=True) * RATE
    es = [jnp.exp2(parts[0] * RATE - top)]
    for c in range(1, CHUNKS):
        es.append(jnp.exp2(parts[c] * RATE - (top if hide is None else top + hide[c])))
    total = fold(es[0], jnp.add)
    for e in es[1:]:
        total = total + fold(e, jnp.add)
    inv = 1.0 / jnp.sum(total, axis=-1, keepdims=True)
    gf = g.astype(F32)
    gs = (gf * inv).astype(BF)
    eb = [e.astype(BF) for e in es]
    zero = jnp.zeros_like(eb[0])
    eb = jnp.concatenate([jnp.where(old, eb[0], zero)] + eb[1:] + [jnp.where(old, zero, eb[0])], axis=1)
    out = (dot(eb, values, 1, 0) * inv).astype(BF)
    delta = jnp.sum(gf * out.astype(F32), axis=-1, keepdims=True) * inv
    dp = dot(gs, values, 1, 1)
    dparts = [jnp.where(old, dp[:, 0:BLOCK], dp[:, WINDOW:SPAN])]
    dparts += [dp[:, c * BLOCK : (c + 1) * BLOCK] for c in range(1, CHUNKS)]
    ds = [(e * (x - delta)).astype(BF) for e, x in zip(es, dparts)]
    ds = jnp.concatenate([jnp.where(old, ds[0], zero)] + ds[1:] + [jnp.where(old, zero, ds[0])], axis=1)
    dq = (dot(ds, keys, 1, 0) * SCALE).astype(BF)
    return out, dq, (q, ds, gs, eb)


def attend_half(qg, row0, ka, a0, kb, b0, hide_when, acc, put, done=None):
    row = lax.broadcasted_iota(jnp.int32, (BLOCK, BLOCK), 0)
    col = lax.broadcasted_iota(jnp.int32, (BLOCK, BLOCK), 1)
    old = col > row
    for b in range(CHUNKS):
        r = b * BLOCK
        keys = jnp.concatenate([ka[a0 + r : a0 + WINDOW, 0:D], kb[b0 : b0 + r + BLOCK, 0:D]], axis=0)
        values = jnp.concatenate([ka[a0 + r : a0 + WINDOW, D : 2 * D], kb[b0 : b0 + r + BLOCK, D : 2 * D]], axis=0)
        hide = None
        if hide_when is not None:
            hide = [jnp.where(hide_when, 1e30, 0.0).astype(F32) if b + c < CHUNKS else 0.0 for c in range(CHUNKS)]
        q = qg[row0 + r : row0 + r + BLOCK, 0:D]
        g = qg[row0 + r : row0 + r + BLOCK, D : 2 * D]
        out, dq, (q, ds, gs, eb) = attend(q, g, keys, values, old, hide)
        put(r, out, dq)
        seen = 0 if b == 0 else WINDOW
        for i, part in enumerate((dot(q, ds, 0, 0), dot(gs, eb, 0, 0))):
            if seen:
                acc[i, :, r : r + seen] += part[:, 0:seen]
            acc[i, :, r + seen : r + SPAN] = part[:, seen:SPAN]
        if done is not None:
            done(r)


def store_rows(ref, row0):
    def put(r, out, dq):
        ref[row0 + r : row0 + r + BLOCK, 0:D] = out
        ref[row0 + r : row0 + r + BLOCK, D : 2 * D] = dq

    return put


def sender(rows, od, row0, acc, sums, sems):
    copies = []

    def send(src, dst):
        copies.append(pltpu.make_async_copy(src, dst, sems.at[len(copies)]))
        copies[-1].start()

    def done(r):
        send(rows.at[pl.ds(r, BLOCK)], od.at[pl.ds(row0 + r, BLOCK), pl.ds(0, 2 * D)])
        if sums is not None:
            cols = pl.ds(r, BLOCK if r + BLOCK < WINDOW else SPAN)
            send(acc.at[:, :, cols], sums.at[:, :, cols])

    return copies, done


def wait_all(copies):
    for copy in copies:
        copy.wait()


LOW, HIGH = slice(0, WINDOW), slice(WINDOW, 2 * WINDOW)
LOW_COLS, HIGH_COLS = pl.ds(0, WINDOW), pl.ds(WINDOW, WINDOW)
GRADS = pl.ds(2 * D, 2 * D)
SCALES = (SCALE, 1.0)


def second_of_first_head(kvqg, od, sums, acc, rows, sems):
    copies, done = sender(rows, od, WINDOW, acc, sums, sems)
    attend_half(kvqg.at[:, 2 * D : 4 * D], WINDOW, kvqg, 0, kvqg, WINDOW, None, acc, store_rows(rows, 0), done)
    wait_all(copies)


def first_of_first_head(lead, kvqg, halo, _, od, sums, acc, rows, sems):
    copies, done = sender(rows, od, 0, acc, sums, sems)
    attend_half(kvqg.at[:, 2 * D : 4 * D], 0, halo, 0, kvqg, 0, lead[0] == 1, acc, store_rows(rows, 0), done)
    wait_all(copies)


def first_of_second_head(lead, kvqg, qg, halo, before, out, back, own, acc, rows, sums, sems):
    load = pltpu.make_async_copy(before.at[:, :, LOW_COLS], sums, sems.at[CHUNKS])
    load.start()
    copies, done = sender(rows, out, 0, acc, None, sems)
    attend_half(qg, 0, halo, 0, kvqg, 0, lead[0] == 1, acc, store_rows(rows, 0), done)
    copies.append(pltpu.make_async_copy(acc.at[:, :, HIGH_COLS], own, sems.at[CHUNKS + 1]))
    copies[-1].start()
    load.wait()
    for i in range(2):
        back[i] = ((acc[i, :, LOW] + sums[i]) * SCALES[i]).astype(BF)
    wait_all(copies)


def second_of_second_head(kvqg, qg, _, sums_s0, sums_f0, sums_f1, out, last, acc, rows, sums, more, most, grads, sems):
    loads = [
        pltpu.make_async_copy(sums_s0, sums, sems.at[CHUNKS]),
        pltpu.make_async_copy(sums_f0.at[:, :, HIGH_COLS], more, sems.at[CHUNKS + 1]),
        pltpu.make_async_copy(sums_f1, most, sems.at[CHUNKS + 2]),
    ]
    for load in loads:
        load.start()
    copies, done = sender(rows, out, WINDOW, acc, None, sems)
    attend_half(qg, WINDOW, kvqg, 0, kvqg, WINDOW, None, acc, store_rows(rows, 0), done)
    wait_all(loads)
    for i in range(2):
        total = (acc[i, :, LOW] + sums[i, :, LOW]) + (more[i] + most[i])
        grads[:, i * D : (i + 1) * D] = (total.T * SCALES[i]).astype(BF)
    copies.append(pltpu.make_async_copy(grads, out.at[LOW_COLS, GRADS], sems.at[CHUNKS + 3]))
    copies[-1].start()
    for i in range(2):
        last[i] = (acc[i, :, HIGH] + sums[i, :, HIGH]) * SCALES[i]
    wait_all(copies)


def join_gradients(last, more, _, out, grads, sem):
    for i in range(2):
        grads[:, i * D : (i + 1) * D] = (last[i] + more[i].astype(F32)).T.astype(BF)
    copy = pltpu.make_async_copy(grads, out.at[HIGH_COLS, GRADS], sem.at[0])
    copy.start()
    copy.wait()


def call(kernel, operands, in_specs, outs, out_specs, scratch, aliases=None):
    pairs = WINDOW * SPAN
    operands = [pltpu.with_memory_space_constraint(x, pltpu.HBM) if spec is AWAY else x for x, spec in zip(operands, in_specs)]
    return pl.pallas_call(
        kernel,
        in_specs=in_specs,
        out_specs=out_specs,
        out_shape=[pltpu.HBM(*out) if spec is AWAY else jax.ShapeDtypeStruct(*out) for out, spec in zip(outs, out_specs)],
        scratch_shapes=[pltpu.VMEM(SUMS, F32)] + scratch + [pltpu.SemaphoreType.DMA((2 * CHUNKS + 1,))],
        input_output_aliases=aliases or {},
        compiler_params=pltpu.CompilerParams(vmem_limit_bytes=20 * 1024 * 1024),
        cost_estimate=cost(12 * pairs * D, 8e6, pairs),
    )(*operands)


def body(queries, keys, values, output_cotangent):
    axes = ("row", "head")
    heads = lax.axis_size("row") * lax.axis_size("head")
    rows = queries.shape[0]
    groups = lax.axis_size("group")
    tokens = heads * rows
    lead = (lax.axis_index("group") == 0).astype(jnp.int32).reshape(1)

    def spread(x):
        return lax.all_to_all(x, axes, split_axis=0, concat_axis=0, tiled=True)

    part = (2, D, WINDOW)
    sums = (SUMS, F32)
    hold = pltpu.VMEM((WINDOW, 2 * D), BF)
    first_cuts = [(0, D, 0, D), (1, D, 0, D), (2, 2 * D, 0, D), (3, 2 * D, 0, D)]
    packed_a = pack([keys, values, queries, output_cotangent], first_cuts, heads)
    packed_b = pack([queries, output_cotangent], [(0, 2 * D, D, D), (1, 2 * D, D, D)], heads)
    kvqg = spread(packed_a).reshape(tokens, 4 * D)
    halo = lax.ppermute(kvqg[tokens - WINDOW :, 0 : 2 * D], "group", [(i, i + 1) for i in range(groups - 1)])
    qg = spread(packed_b).reshape(tokens, 2 * D)
    od_0, sums_s0 = call(second_of_first_head, [kvqg], [VMEM], [((tokens, 2 * D), BF), sums], [AWAY, AWAY], [hold])
    od_0, sums_f0 = call(
        first_of_first_head,
        [lead, kvqg, halo, od_0],
        [SMEM, VMEM, VMEM, AWAY],
        [((tokens, 2 * D), BF), sums],
        [AWAY, AWAY],
        [hold],
        {3: 0},
    )
    out, back, own = call(
        first_of_second_head,
        [lead, kvqg, qg, halo, sums_f0],
        [SMEM, VMEM, VMEM, VMEM, AWAY],
        [((tokens, 4 * D), BF), (part, BF), (part, F32)],
        [AWAY, VMEM, AWAY],
        [hold, pltpu.VMEM(part, F32)],
    )
    more = lax.ppermute(back, "group", [(i + 1, i) for i in range(groups - 1)])
    chunks_a = spread(od_0.reshape(heads, rows, 2 * D))
    out, last = call(
        second_of_second_head,
        [kvqg, qg, out, sums_s0, sums_f0, own],
        [VMEM, VMEM, AWAY, AWAY, AWAY, AWAY],
        [((tokens, 4 * D), BF), (part, F32)],
        [AWAY, VMEM],
        [hold, pltpu.VMEM(SUMS, F32), pltpu.VMEM(part, F32), pltpu.VMEM(part, F32), hold],
        {2: 0},
    )
    out = pl.pallas_call(
        join_gradients,
        in_specs=[VMEM, VMEM, AWAY],
        out_specs=AWAY,
        out_shape=pltpu.HBM(out.shape, BF),
        scratch_shapes=[hold, pltpu.SemaphoreType.DMA((1,))],
        input_output_aliases={2: 0},
        compiler_params=pltpu.CompilerParams(vmem_limit_bytes=20 * 1024 * 1024),
        cost_estimate=cost(0, 4e6),
        name="join_gradients",
    )(last, more, pltpu.with_memory_space_constraint(out, pltpu.HBM))
    chunks_b = spread(out.reshape(heads, rows, 4 * D))
    chunks_a = stage(chunks_a)
    return unpack(
        [chunks_a, chunks_b],
        [[(0, 2 * D, 0, D), (1, 2 * D, 0, D)], [(0, 2 * D, D, D), (1, 2 * D, D, D), (2, D, 0, D), (3, D, 0, D)]],
        [2 * D, 2 * D, D, D],
    )


def solution(mesh):
    row = 4
    seq, head = mesh.devices.shape
    finer = Mesh(mesh.devices.reshape(seq // row, row, head), ("group", "row", "head"))
    spec = P(("group", "row", "head"), None)
    return jax.shard_map(body, mesh=finer, in_specs=(spec,) * 4, out_specs=(spec,) * 4, check_vma=False)
```
